768 devices in a mesh: depth: 8 (over y), row: 2 (over core), col: 48 (over z, x).
Axes of the slice: x: 4, y: 8, z: 12, core: 2. Of those that a mesh axis runs over, the one named last changes fastest.
Arguments:
- density: float32 [128, 256, 6144], P('depth', 'row', 'col'), may hold values from 0.002 to 0.05
- albedo: bfloat16 [3, 128, 256, 6144], P(None, 'depth', 'row', 'col'), may hold values from 0.099609375 to 1
- targets: int32 [2, 8, 2, 48], P(None, None, 'row'), may hold values from -1 to 50, as said below
- offsets: int32 [2, 8, 2, 48], P(None, None, 'row', 'col'), may hold values from 0 to 127
- slab_order: int32 [2, 8], replicated, may hold values from 0 to 7, each once within a row
Outputs:
- frame: float32 [2, 4, 2, 128, 6144], P(None, None, 'row', 'depth', 'col')
The draws below stay inside these ranges and needn't reach their ends.
Inputs may be any that keep to these rules, and one draw needn't show every extreme that they name: `targets`: within one view and one row and column c of bricks, the 8 values are c + b, c + b, c + b + 1, c + b + 1, ... assigned to the slabs in some order (two bricks for each value, b is -1 or 0; b is -1 in column 0 and 0 in the last column), so one column of bricks sends at most 4 pieces to one screen tile, a number reached in every view, row and column, and only to tiles c - 1 .. c + 4.
All inputs are finite; a program needn't handle non-finite values.
Results may differ from the reference program's by a relative error of at most 0.0015.
Values may be sent and summed in bfloat16 or wider, within the bound.
A program may use at most 32 MiB of HBM per device.

```python
import math
import jax
import jax.numpy as jnp
from jax import lax

VIEWS = 2
BD = 16
BR = 128
BC = 128
NZ = 128
NY = 256
NX = 6144
N_DEPTH = 8
N_ROW = 2
N_COL = 48


def draw_targets(key, part):
    streams = jax.random.split(jax.random.fold_in(key, 11), 2)
    scores = jax.random.randint(streams[0], (VIEWS, N_ROW, N_COL, N_DEPTH), 0, 1 << 20)
    distinct = scores * N_DEPTH + jnp.arange(N_DEPTH, dtype=jnp.int32)
    ranks = jnp.argsort(jnp.argsort(distinct, axis=-1), axis=-1).astype(jnp.int32)
    relative = ranks // 2
    base_tile = jax.random.randint(streams[1], (VIEWS, N_ROW, N_COL), -1, 1)
    column_ids = jnp.arange(N_COL, dtype=jnp.int32)[None, None, :]
    base_tile = jnp.where(column_ids == 0, -1, base_tile)
    base_tile = jnp.where(column_ids == N_COL - 1, 0, base_tile)
    result = (column_ids + base_tile)[..., None] + relative
    return result.transpose(0, 3, 1, 2).astype(jnp.int32)


def touch_ends(values, stream_key, smallest, largest):
    longest = values.shape.index(max(values.shape))
    spots = []
    for shift in (0, 1):
        where = [jax.random.randint(jax.random.fold_in(stream_key, axis), (), 0, length) for axis, length in enumerate(values.shape)]
        where[longest] = (where[longest] + shift) % values.shape[longest]
        spots.append(tuple(where))
    return values.at[spots[0]].set(smallest).at[spots[1]].set(largest)


def steps_of(key, extent, cuts, smallest, high):
    level, own = 1.0, jax.random.fold_in(key, 6)
    for dim, parts in cuts:
        heights = jnp.exp(jax.random.uniform(jax.random.fold_in(own, dim), (parts,), jnp.float32, smallest / len(cuts), high / len(cuts)))
        level = level * jnp.repeat(heights, extent[dim] // parts).reshape([-1 if axis == dim else 1 for axis in range(len(extent))])
    return level


def setup_inputs(seed: int = 0) -> dict:
    key_of = jax.random.split(jax.random.key(seed), 6)
    density = jnp.clip(jnp.exp(math.log(0.05) - 3.218876 * jax.random.uniform(key_of[0], (NZ, NY, NX), jnp.float32) ** steps_of(key_of[0], (NZ, NY, NX), ((0, 8), (1, 2), (2, 48)), -0.2, 0.2)), 0.002, 0.05)
    albedo = jnp.clip(0.099609375 + 0.9003906 * jax.random.uniform(key_of[1], (3, NZ, NY, NX), jnp.float32) ** steps_of(key_of[1], (3, NZ, NY, NX), ((1, 8), (2, 2), (3, 48)), -0.2, 0.2), 0.099609375, 1.0).astype(jnp.bfloat16)
    targets = draw_targets(jax.random.fold_in(key_of[5], 71), 0)
    offsets = touch_ends(jax.random.randint(key_of[3], (VIEWS, N_DEPTH, N_ROW, N_COL), 0, BC), jax.random.fold_in(key_of[3], 1), 0, BC - 1).astype(jnp.int32)
    slab_order = jax.vmap(lambda own: jax.random.permutation(own, N_DEPTH))(jax.random.split(key_of[4], VIEWS)).reshape((VIEWS, N_DEPTH)).astype(jnp.int32)
    return {"density": density, "albedo": albedo, "targets": targets, "offsets": offsets, "slab_order": slab_order}


SHEARS = (0.3125, -0.4375)
BRIGHTNESS = 4.0


def shear_columns(values, shear, plane_index, margin):
    integer_part = math.floor(shear * plane_index)
    fraction = shear * plane_index - integer_part
    col_count = values.shape[-1]
    padding = [(0, 0)] * (values.ndim - 1) + [(margin, margin)]
    padded = jnp.pad(values, padding)
    nearer = padded[..., margin - integer_part:margin - integer_part + col_count]
    farther = padded[..., margin - integer_part - 1:margin - integer_part - 1 + col_count]
    return (1.0 - fraction) * nearer + fraction * farther


def composite_slabs(premult, shear):
    depth_cells = premult.shape[2]
    colour_sum = jnp.zeros((3,) + premult.shape[1:2] + premult.shape[3:], jnp.float32)
    transmit = jnp.ones(premult.shape[1:2] + premult.shape[3:], jnp.float32)
    for plane_index in range(depth_cells):
        moved = shear_columns(premult[:, :, plane_index], shear, plane_index, depth_cells + 2)
        colour_sum = colour_sum + transmit[None] * moved[:3]
        transmit = transmit * (1.0 - moved[3])
    return jnp.concatenate([colour_sum, (1.0 - transmit)[None]], axis=0).astype(jnp.bfloat16)


def render_row(row_density, row_albedo):
    blocks = row_density.reshape(N_DEPTH, BD, BR, NX)
    slab_plane = jnp.exp(-jnp.sum(blocks, axis=1))
    ahead = jnp.concatenate([jnp.ones((1, BR, NX), jnp.float32), jnp.cumprod(slab_plane, axis=0)[:-1]], axis=0)
    in_front = jnp.cumsum(blocks, axis=1) - blocks
    lighting = ahead[:, None] * jnp.exp(-in_front)
    opacity = 1.0 - jnp.exp(-blocks)
    colour = BRIGHTNESS * row_albedo.reshape(3, N_DEPTH, BD, BR, NX).astype(jnp.float32) * (lighting * opacity)[None]
    premult = jnp.concatenate([colour, opacity[None]], axis=0).reshape(4, N_DEPTH, BD, BR, N_COL, BC)
    return jnp.stack([composite_slabs(premult, shear) for shear in SHEARS])


def place_piece(colour_row, log_row, piece_row, start_col):
    seg_log = lax.dynamic_slice_in_dim(log_row, start_col, BC, 1)
    seg_colour = lax.dynamic_slice_in_dim(colour_row, start_col, BC, 2)
    values = piece_row.astype(jnp.float32)
    seg_colour = seg_colour + jnp.exp(seg_log)[None] * values[:3]
    seg_log = seg_log + jnp.log1p(-values[3])
    return (lax.dynamic_update_slice_in_dim(colour_row, seg_colour, start_col, 2),
            lax.dynamic_update_slice_in_dim(log_row, seg_log, start_col, 1))


def reference(density, albedo, targets, offsets, slab_order):
    row_density = density.reshape(NZ, N_ROW, BR, NX).transpose(1, 0, 2, 3)
    row_albedo = albedo.reshape(3, NZ, N_ROW, BR, NX).transpose(2, 0, 1, 3, 4)
    pictures = lax.map(lambda pair: render_row(pair[0], pair[1]), (row_density, row_albedo))
    pad_width = (N_COL + N_DEPTH + 3) * BC
    frames = []
    for view_index in range(VIEWS):
        view_pictures = pictures[:, view_index]

        def place_step(step_index, state):
            position = step_index // N_COL
            column = step_index % N_COL
            slab = slab_order[view_index, position]
            chosen = lax.dynamic_index_in_dim(view_pictures, slab, axis=2, keepdims=False)
            chosen = lax.dynamic_index_in_dim(chosen, column, axis=3, keepdims=False)
            start_cols = ((targets[view_index, slab, :, column] + 1) * BC + offsets[view_index, slab, :, column]).astype(jnp.int32)
            return jax.vmap(place_piece)(state[0], state[1], chosen, start_cols)

        colour_start = jnp.zeros((N_ROW, 3, BR, pad_width), jnp.float32)
        log_start = jnp.zeros((N_ROW, BR, pad_width), jnp.float32)
        colour_sum, log_sum = lax.fori_loop(0, N_DEPTH * N_COL, place_step, (colour_start, log_start))
        colour_sum = colour_sum[..., BC:BC + NX]
        opacity = 1.0 - jnp.exp(log_sum[..., BC:BC + NX])
        frames.append(jnp.concatenate([colour_sum, opacity[:, None]], axis=1).transpose(1, 0, 2, 3))
    return jnp.stack(frames)
```

```python
import functools
import math

import jax
import jax.numpy as jnp
from jax import lax
from jax.experimental import pallas as pl
from jax.experimental.pallas import tpu as pltpu
from jax.sharding import PartitionSpec as P

SHEARS = (0.3125, -0.4375)
BRIGHTNESS = 4.0
MESH = pl.DeviceIdType.MESH

STEPS = (-1, 0, 1, 2, 3, 4)
SLOT_COUNT = {-1: 2, 0: 4, 1: 4, 2: 4, 3: 4, 4: 2}
SLOT_BASE = {-1: 0, 0: 2, 1: 6, 2: 10, 3: 14, 4: 18}
SLOTS = 20
EMPTY = 20


def shear_plan(shear, depth_cells):
    plan = []
    for z in range(depth_cells):
        whole = math.floor(shear * z)
        plan.append((whole, shear * z - whole))
    terms = sorted({k + e for k, f in plan for e in (0, 1) if e == 0 or f > 0})
    return plan, terms


def kernel(
    sizes,
    density_hbm,
    albedo_hbm,
    targets,
    offsets,
    slab_order,
    out_ref,
    dens,
    alb,
    depth_strips,
    depth_seen,
    light_strips,
    light,
    partial,
    images,
    strips_a,
    strips_b,
    outgoing,
    landed_a,
    landed_b,
    table,
    load_sems,
    a_send,
    a_recv,
    b_send,
    b_recv,
    y_send,
    y_recv,
    c_send,
    c_recv,
):
    slabs, columns, depth_cells, rows, lanes = sizes
    views = len(SHEARS)
    strips, landed = (strips_a, strips_b), (landed_a, landed_b)
    strip = rows // slabs
    plans = [shear_plan(shear, depth_cells) for shear in SHEARS]
    firsts = [0, len(plans[0][1])]
    me = lax.axis_index("depth")
    col = lax.axis_index("col")

    load_density = pltpu.make_async_copy(density_hbm, dens, load_sems.at[0])
    load_albedo = pltpu.make_async_copy(albedo_hbm, alb, load_sems.at[1])
    load_density.start()
    load_albedo.start()

    barrier = pltpu.get_barrier_semaphore()
    for hop in range(1, slabs):
        pl.semaphore_signal(
            barrier, inc=1, device_id={"depth": lax.rem(me + hop, slabs)}, device_id_type=MESH
        )
    for hop in (-4, -3, -2, -1, 1, 2, 3, 4):

        @pl.when((col + hop >= 0) & (col + hop < columns))
        def _(hop=hop):
            pl.semaphore_signal(
                barrier, inc=1, device_id={"col": col + hop}, device_id_type=MESH
            )

    lane = lax.broadcasted_iota(jnp.int32, (strip, lanes), 1)

    def strip_rows(p):
        return pl.ds(pl.multiple_of(p * strip, strip), strip)

    load_density.wait()

    @pl.loop(0, slabs)
    def _(p):
        depth_strips[p] = jnp.sum(dens[:, strip_rows(p), :], axis=0)

    neighbours = jnp.minimum(col, 4) + jnp.minimum(columns - 1 - col, 4)
    pl.semaphore_wait(barrier, slabs - 1 + neighbours)

    def peer_at(i):
        half, sign = (i + 1) // 2, 1 - 2 * (i % 2)
        return lax.rem(me + slabs // 2 + sign * half, slabs)

    def depth_copy(src, dst, send, recv, slot_send, slot_recv, peer):
        return pltpu.make_async_remote_copy(
            src_ref=src,
            dst_ref=dst,
            send_sem=send.at[slot_send],
            recv_sem=recv.at[slot_recv],
            device_id={"depth": peer},
            device_id_type=MESH,
        )

    def a_copy(peer, source):
        return depth_copy(
            depth_strips.at[peer], depth_seen.at[source], a_send, a_recv, peer, source, peer
        )

    def b_copy(peer, source):
        return depth_copy(
            light_strips.at[peer], light.at[source], b_send, b_recv, peer, source, peer
        )

    @pl.loop(0, slabs - 1)
    def _(i):
        a_copy(peer_at(i), me).start()

    depth_seen[me] = depth_strips[me]
    load_albedo.wait()

    def lane_mask(shift, weight):
        inside = (lane >= shift) if shift >= 0 else (lane < lanes + shift)
        return jnp.where(inside, jnp.float32(weight), jnp.float32(0.0))

    def rolled(value, shift):
        return value if shift % lanes == 0 else pltpu.roll(value, shift % lanes, 1)

    def composite(p):
        at = strip_rows(p)
        inside = jnp.ones((strip, lanes), jnp.float32)
        transmit = [jnp.ones((strip, lanes), jnp.float32) for _ in range(views)]
        sums = [{} for _ in range(views)]
        for z in range(depth_cells):
            through = jnp.exp(-dens[z, at, :])
            opacity = 1.0 - through
            lit = (BRIGHTNESS * inside) * opacity
            inside = inside * through
            colour = [alb[c, z, at, :].astype(jnp.float32) * lit for c in range(3)]
            for v in range(views):
                whole, fraction = plans[v][0][z]
                moved = None
                for k, weight in ((whole, 1.0 - fraction), (whole + 1, fraction)):
                    if weight == 0.0:
                        continue
                    part = lane_mask(k, weight) * rolled(opacity, k)
                    moved = part if moved is None else moved + part
                    seen = transmit[v] if z else None
                    seen = lane_mask(-k, weight) * (
                        rolled(seen, -k) if z else jnp.ones((strip, lanes), jnp.float32)
                    )
                    terms = [seen * colour[c] for c in range(3)]
                    if k in sums[v]:
                        terms = [old + new for old, new in zip(sums[v][k], terms)]
                    sums[v][k] = terms
                transmit[v] = transmit[v] * (1.0 - moved)
                later = {
                    k for w, f in plans[v][0][z + 1 :] for k in ((w, w + 1) if f else (w,))
                }
                for k in [k for k in sums[v] if k not in later]:
                    for c in range(3):
                        partial[firsts[v] + plans[v][1].index(k), c, at, :] = sums[v][k][c]
                    del sums[v][k]
        for v in range(views):
            image = pltpu.roll(1.0 - transmit[v], offsets[v, 0, 0, me], 1)
            images[v, p, 3] = image.astype(jnp.bfloat16)

    early = slabs // 2
    pl.loop(0, early)(composite)

    @pl.loop(0, slabs - 1)
    def _(i):
        a_copy(me, peer_at(i)).wait_recv()

    front = jnp.zeros((strip, lanes), jnp.float32)
    for d in range(slabs):
        light_strips[d] = jnp.exp(-front)
        front = front + depth_seen[d]

    @pl.loop(0, slabs - 1)
    def _(i):
        b_copy(peer_at(i), me).start()

    light[me] = light_strips[me]

    pl.loop(early, slabs)(composite)

    for v in range(views):
        for n, step in enumerate(STEPS):
            source = col - step
            present = (source >= 0) & (source < columns)
            source = jnp.clip(source, 0, columns - 1)
            rel = [targets[v, d, 0, source] - source for d in range(slabs)]
            for d in range(slabs):
                second = functools.reduce(
                    jnp.logical_or, [rel[e] == rel[d] for e in range(d)], False
                )
                member = jnp.where(second, 1, 0)
                slot = jnp.int32(EMPTY)
                if step < 4:
                    slot = jnp.where(rel[d] == step, SLOT_BASE[step] + member, slot)
                if step > -1:
                    after = SLOT_BASE[step] + (2 if step < 4 else 0)
                    slot = jnp.where(rel[d] == step - 1, after + member, slot)
                table[v, n, d] = jnp.where(present, slot, EMPTY)

    @pl.loop(0, slabs - 1)
    def _(i):
        b_copy(me, peer_at(i)).wait_recv()

    def y_copy(v, peer, source):
        return depth_copy(
            images.at[v, peer],
            strips[v].at[source],
            y_send.at[v],
            y_recv.at[v],
            peer,
            source,
            peer,
        )

    for v in range(views):

        @pl.loop(0, slabs)
        def _(i, v=v):
            p = peer_at(i)
            at = strip_rows(p)
            front_light = light[p]
            for c in range(3):
                total = None
                for n, k in enumerate(plans[v][1]):
                    part = rolled(front_light * partial[firsts[v] + n, c, at, :], k)
                    total = part if total is None else total + part
                total = pltpu.roll(total, offsets[v, 0, 0, me], 1)
                images[v, p, c] = total.astype(jnp.bfloat16)

            @pl.when(i < slabs - 1)
            def _():
                y_copy(v, p, me).start()

        strips[v][me] = images[v, me]

    def c_copy(v, step):
        base, count = SLOT_BASE[step], SLOT_COUNT[step]
        n = STEPS.index(step)
        return pltpu.make_async_remote_copy(
            src_ref=outgoing.at[v, pl.ds(base, count)],
            dst_ref=landed[v].at[pl.ds(base, count)],
            send_sem=c_send.at[v, n],
            recv_sem=c_recv.at[v, n],
            device_id={"col": col + step},
            device_id_type=MESH,
        )

    for v in range(views):
        landed[v][EMPTY] = jnp.zeros(landed[v].shape[1:], jnp.bfloat16)

        @pl.loop(0, slabs - 1)
        def _(i, v=v):
            y_copy(v, me, peer_at(i)).wait_recv()

        rel = [targets[v, d, 0, col] - col for d in range(slabs)]
        for step in (3, 2, 1, 0, -1):
            match = [r == step for r in rel]
            first = jnp.int32(slabs)
            second = jnp.int32(-1)
            for d in range(slabs):
                first = jnp.where(match[d], jnp.minimum(first, d), first)
                second = jnp.where(match[d], d, second)
            valid = second >= 0
            for member, slab in ((0, first), (1, second)):
                slab = jnp.where(valid, slab, 0)
                start = offsets[v, 0, 0, slab]
                piece = strips[v][slab]
                left_from = jnp.where(valid, start, lanes)
                right_to = jnp.where(valid, start, 0)
                left = jnp.where(lane >= left_from, 1.0, 0.0).astype(jnp.bfloat16)
                right = jnp.where(lane < right_to, 1.0, 0.0).astype(jnp.bfloat16)
                after = step + 1
                slots_of = [landed[v] if s == 0 else outgoing.at[v] for s in (step, after)]
                slots_of[0][SLOT_BASE[step] + member] = piece * left
                slots_of[1][SLOT_BASE[after] + (2 if after < 4 else 0) + member] = piece * right
            for ready in ((4,) if step == 3 else (step + 1,)) + ((-1,) if step == -1 else ()):
                if ready == 0:
                    continue

                @pl.when((col + ready >= 0) & (col + ready < columns))
                def _(v=v, ready=ready):
                    c_copy(v, ready).start()

    for v in range(views):
        for step in STEPS:
            if step == 0:
                continue

            @pl.when((col - step >= 0) & (col - step < columns))
            def _(v=v, step=step):
                c_copy(v, step).wait_recv()

        def at_position(position, state, v=v):
            slab = slab_order[v, position]
            red, green, blue, transmit = state
            for n in reversed(range(len(STEPS))):
                piece = landed[v][table[v, n, slab]].astype(jnp.float32)
                red = red + transmit * piece[0]
                green = green + transmit * piece[1]
                blue = blue + transmit * piece[2]
                transmit = transmit * (1.0 - piece[3])
            return red, green, blue, transmit

        zero = jnp.zeros((strip, lanes), jnp.float32)
        red, green, blue, transmit = lax.fori_loop(
            0, slabs, at_position, (zero, zero, zero, zero + 1.0)
        )
        out_ref[v, 0, 0] = red
        out_ref[v, 1, 0] = green
        out_ref[v, 2, 0] = blue
        out_ref[v, 3, 0] = 1.0 - transmit

    @pl.loop(0, slabs - 1)
    def _(i):
        peer = peer_at(i)
        a_copy(peer, me).wait_send()
        b_copy(peer, me).wait_send()
        for v in range(views):
            y_copy(v, peer, me).wait_send()

    for v in range(views):
        for step in STEPS:
            if step == 0:
                continue

            @pl.when((col + step >= 0) & (col + step < columns))
            def _(v=v, step=step):
                c_copy(v, step).wait_send()


def on_device(density, albedo, targets, offsets, slab_order):
    depth_cells, rows, lanes = density.shape
    views = slab_order.shape[0]
    slabs = lax.axis_size("depth")
    columns = lax.axis_size("col")
    strip = rows // slabs
    terms = sum(len(shear_plan(shear, depth_cells)[1]) for shear in SHEARS)
    f32, bf16 = jnp.float32, jnp.bfloat16
    dma = pltpu.SemaphoreType.DMA
    return pl.pallas_call(
        functools.partial(kernel, (slabs, columns, depth_cells, rows, lanes)),
        out_shape=jax.ShapeDtypeStruct((views, 4, 1, strip, lanes), f32),
        in_specs=[
            pl.BlockSpec(memory_space=pl.ANY),
            pl.BlockSpec(memory_space=pl.ANY),
            pl.BlockSpec(memory_space=pltpu.SMEM),
            pl.BlockSpec(memory_space=pltpu.SMEM),
            pl.BlockSpec(memory_space=pltpu.SMEM),
        ],
        out_specs=pl.BlockSpec(memory_space=pltpu.VMEM),
        scratch_shapes=[
            pltpu.VMEM((depth_cells, rows, lanes), f32),
            pltpu.VMEM((3, depth_cells, rows, lanes), bf16),
            pltpu.VMEM((slabs, strip, lanes), f32),
            pltpu.VMEM((slabs, strip, lanes), f32),
            pltpu.VMEM((slabs, strip, lanes), f32),
            pltpu.VMEM((slabs, strip, lanes), f32),
            pltpu.VMEM((terms, 3, rows, lanes), f32),
            pltpu.VMEM((views, slabs, 4, strip, lanes), bf16),
            pltpu.VMEM((slabs, 4, strip, lanes), bf16),
            pltpu.VMEM((slabs, 4, strip, lanes), bf16),
            pltpu.VMEM((views, SLOTS, 4, strip, lanes), bf16),
            pltpu.VMEM((SLOTS + 1, 4, strip, lanes), bf16),
            pltpu.VMEM((SLOTS + 1, 4, strip, lanes), bf16),
            pltpu.SMEM((views, len(STEPS), slabs), jnp.int32),
            dma((2,)),
            dma((slabs,)),
            dma((slabs,)),
            dma((slabs,)),
            dma((slabs,)),
            dma((views, slabs)),
            dma((views, slabs)),
            dma((views, len(STEPS))),
            dma((views, len(STEPS))),
        ],
        compiler_params=pltpu.CompilerParams(collective_id=0, has_side_effects=True),
    )(density, albedo, targets, offsets.transpose(0, 2, 3, 1), slab_order)


def solution(mesh):
    in_specs = (
        P("depth", "row", "col"),
        P(None, "depth", "row", "col"),
        P(None, None, "row", None),
        P(None, None, "row", "col"),
        P(),
    )
    out_specs = P(None, None, "row", "depth", "col")
    return jax.shard_map(
        on_device, mesh=mesh, in_specs=in_specs, out_specs=out_specs, check_vma=False
    )
```

```python
import functools
import math

import jax
import jax.numpy as jnp
from jax import lax
from jax.experimental import pallas as pl
from jax.experimental.pallas import tpu as pltpu
from jax.sharding import PartitionSpec as P

SHEARS = (0.3125, -0.4375)
BRIGHTNESS = 4.0
LOGICAL = pl.DeviceIdType.LOGICAL
MIDDLE = 0.29

STEPS = (-1, 0, 1, 2, 3, 4)
SLOT_COUNT = {-1: 2, 0: 4, 1: 4, 2: 4, 3: 4, 4: 2}
SLOT_BASE = {-1: 0, 0: 2, 1: 6, 2: 10, 3: 14, 4: 18}
SLOTS = 20
EMPTY = 20
EARLY = 4
UNROLL = 2


def shear_plan(shear, depth_cells):
    plan = []
    for z in range(depth_cells):
        whole = math.floor(shear * z)
        plan.append((whole, shear * z - whole))
    terms = sorted({k + e for k, f in plan for e in (0, 1) if e == 0 or f > 0})
    return plan, terms


def kernel(
    sizes,
    density_hbm,
    albedo_hbm,
    targets_hbm,
    offsets_hbm,
    order_hbm,
    out_ref,
    targets,
    offsets,
    slab_order,
    dens,
    alb,
    depth_strips,
    depth_seen,
    light_strips,
    light,
    partial,
    images,
    veils,
    strips_a,
    strips_b,
    veil_strips,
    outgoing,
    veil_outgoing,
    landed_a,
    landed_b,
    veil_landed,
    table,
    picks,
    density_sems,
    load_sems,
    a_send,
    a_recv,
    b_send,
    b_recv,
    o_send,
    o_recv,
    y_send,
    y_recv,
    c_send,
    c_recv,
):
    slabs, columns, depth_cells, rows, lanes = sizes
    views = len(SHEARS)
    strips, landed = (strips_a, strips_b), (landed_a, landed_b)
    strip = rows // slabs
    plans = [shear_plan(shear, depth_cells) for shear in SHEARS]
    firsts = [0, len(plans[0][1])]
    me = lax.axis_index("depth")
    col = lax.axis_index("col")
    layer = lax.axis_size("row") * columns
    here = me * layer + lax.axis_index("row") * columns + col

    def device(peer):
        return here + (peer - me) * layer


    barrier = pltpu.get_barrier_semaphore()
    for hop in range(1, slabs):
        pl.semaphore_signal(
            barrier,
            inc=1,
            device_id=device(lax.rem(me + hop, slabs)),
            device_id_type=LOGICAL,
        )
    for hop in (-4, -3, -2, -1, 1, 2, 3, 4):

        @pl.when((col + hop >= 0) & (col + hop < columns))
        def _(hop=hop):
            pl.semaphore_signal(barrier, inc=1, device_id=here + hop, device_id_type=LOGICAL)

    lane = lax.broadcasted_iota(jnp.int32, (strip, lanes), 1)

    def strip_rows(p):
        return pl.ds(pl.multiple_of(p * strip, strip), strip)

    def peer_at(i):
        half, sign = (i + 1) // 2, 1 - 2 * (i % 2)
        return lax.rem(me + slabs // 2 + sign * half, slabs)

    def density_load(i):
        at = strip_rows(peer_at(i))
        return pltpu.make_async_copy(density_hbm.at[:, at], dens.at[:, at], density_sems.at[i])

    @pl.loop(0, slabs)
    def _(i):
        density_load(i).start()

    load_small = [
        pltpu.make_async_copy(src, dst, load_sems.at[n])
        for n, (src, dst) in enumerate(
            ((offsets_hbm, offsets), (targets_hbm, targets), (order_hbm, slab_order))
        )
    ]
    for load in load_small:
        load.start()
    load_albedo = pltpu.make_async_copy(albedo_hbm, alb, load_sems.at[3])
    load_albedo.start()

    neighbours = jnp.minimum(col, 4) + jnp.minimum(columns - 1 - col, 4)
    pl.semaphore_wait(barrier, slabs - 1 + neighbours)

    def depth_copy(src, dst, send_sem, recv_sem, peer):
        return pltpu.make_async_remote_copy(
            src_ref=src,
            dst_ref=dst,
            send_sem=send_sem,
            recv_sem=recv_sem,
            device_id=device(peer),
            device_id_type=LOGICAL,
        )

    def all_peers(src, dst, send_sem, recv_sem):
        span = pl.ds(0, slabs - 1)
        return depth_copy(src.at[span], dst.at[span], send_sem, recv_sem, me)

    def a_copy(peer, source):
        return depth_copy(depth_strips.at[peer], depth_seen.at[source], a_send, a_recv, peer)

    def b_copy(peer, source):
        return depth_copy(light_strips.at[peer], light.at[source], b_send, b_recv, peer)

    def all_a():
        return all_peers(depth_strips, depth_seen, a_send, a_recv)

    def all_b():
        return all_peers(light_strips, light, b_send, b_recv)

    @pl.loop(0, slabs)
    def _(i):
        p = peer_at(i)
        density_load(i).wait()
        total = jnp.sum(dens[:, strip_rows(p), :], axis=0)
        depth_strips[p] = (total - MIDDLE).astype(jnp.bfloat16)

        @pl.when(i < slabs - 1)
        def _():
            a_copy(p, me).start()

    depth_seen[me] = depth_strips[me]
    for load in load_small:
        load.wait()
    load_albedo.wait()

    def lane_mask(shift, weight):
        inside = (lane >= shift) if shift >= 0 else (lane < lanes + shift)
        return jnp.where(inside, jnp.float32(weight), jnp.float32(0.0))

    def rolled(value, shift):
        return value if shift % lanes == 0 else pltpu.roll(value, shift % lanes, 1)

    def o_copy(peer, source):
        return depth_copy(veils.at[peer], veil_strips.at[source], o_send, o_recv, peer)

    def composite(i):
        p = peer_at(i)
        at = strip_rows(p)
        inside = jnp.ones((strip, lanes), jnp.float32)
        transmit = [jnp.ones((strip, lanes), jnp.float32) for _ in range(views)]
        sums = [{} for _ in range(views)]
        for z in range(depth_cells):
            through = jnp.exp(-dens[z, at, :])
            opacity = 1.0 - through
            lit = (BRIGHTNESS * inside) * opacity
            inside = inside * through
            colour = [alb[c, z, at, :].astype(jnp.float32) * lit for c in range(3)]
            for v in range(views):
                whole, fraction = plans[v][0][z]
                moved = None
                for k, weight in ((whole, 1.0 - fraction), (whole + 1, fraction)):
                    if weight == 0.0:
                        continue
                    part = lane_mask(k, weight) * rolled(opacity, k)
                    moved = part if moved is None else moved + part
                    seen = transmit[v] if z else None
                    seen = lane_mask(-k, weight) * (
                        rolled(seen, -k) if z else jnp.ones((strip, lanes), jnp.float32)
                    )
                    terms = [seen * colour[c] for c in range(3)]
                    if k in sums[v]:
                        terms = [old + new for old, new in zip(sums[v][k], terms)]
                    sums[v][k] = terms
                transmit[v] = transmit[v] * (1.0 - moved)
                later = {
                    k for w, f in plans[v][0][z + 1 :] for k in ((w, w + 1) if f else (w,))
                }
                for k in [k for k in sums[v] if k not in later]:
                    for c in range(3):
                        partial[firsts[v] + plans[v][1].index(k), c, at, :] = sums[v][k][c]
                    del sums[v][k]
        for v in range(views):
            image = pltpu.roll(1.0 - transmit[v], offsets[v, 0, 0, me], 1)
            veils[p, v] = image.astype(jnp.bfloat16)

        @pl.when(i < slabs - 1)
        def _():
            o_copy(p, me).start()

    pl.loop(0, EARLY)(composite)
    all_a().wait_recv()
    before = jnp.zeros((strip, lanes), jnp.float32)
    for d in range(slabs):
        light_strips[d] = jnp.exp(-before).astype(jnp.bfloat16)
        before = before + (depth_seen[d].astype(jnp.float32) + MIDDLE)

    @pl.loop(0, slabs - 1)
    def _(i):
        b_copy(peer_at(i), me).start()

    light[me] = light_strips[me]
    pl.loop(EARLY, slabs)(composite)
    veil_strips[me] = veils[me]

    for v in range(views):
        rel = [targets[v, d, 0, col] - col for d in range(slabs)]
        for n, step in enumerate(STEPS[:-1]):
            first = jnp.int32(slabs)
            second = jnp.int32(-1)
            for d in range(slabs):
                match = rel[d] == step
                first = jnp.where(match, jnp.minimum(first, d), first)
                second = jnp.where(match, d, second)
            valid = second >= 0
            for member, slab in ((0, first), (1, second)):
                slab = jnp.where(valid, slab, 0)
                start = offsets[v, 0, 0, slab]
                picks[v, n, member, 0] = slab
                picks[v, n, member, 1] = jnp.where(valid, start, lanes)
                picks[v, n, member, 2] = jnp.where(valid, start, 0)

    for v in range(views):
        for n, step in enumerate(STEPS):
            source = col - step
            present = (source >= 0) & (source < columns)
            source = jnp.clip(source, 0, columns - 1)
            rel = [targets[v, d, 0, source] - source for d in range(slabs)]
            for d in range(slabs):
                second = functools.reduce(
                    jnp.logical_or, [rel[e] == rel[d] for e in range(d)], False
                )
                member = jnp.where(second, 1, 0)
                slot = jnp.int32(EMPTY)
                if step < 4:
                    slot = jnp.where(rel[d] == step, SLOT_BASE[step] + member, slot)
                if step > -1:
                    after = SLOT_BASE[step] + (2 if step < 4 else 0)
                    slot = jnp.where(rel[d] == step - 1, after + member, slot)
                table[v, n, d] = jnp.where(present, slot, EMPTY)

    all_b().wait_recv()

    def y_copy(v, peer, source):
        return depth_copy(
            images.at[v, peer], strips[v].at[source], y_send.at[v], y_recv.at[v], peer
        )

    def all_o():
        return all_peers(veils, veil_strips, o_send, o_recv)

    def all_y(v):
        return all_peers(images.at[v], strips[v], y_send.at[v], y_recv.at[v])

    for v in range(views):

        @pl.loop(0, slabs, unroll=UNROLL)
        def _(i, v=v):
            p = peer_at(i)
            at = strip_rows(p)
            front_light = light[p].astype(jnp.float32)
            for c in range(3):
                total = None
                for n, k in enumerate(plans[v][1]):
                    part = rolled(front_light * partial[firsts[v] + n, c, at, :], k)
                    total = part if total is None else total + part
                total = pltpu.roll(total, offsets[v, 0, 0, me], 1)
                images[v, p, c] = total.astype(jnp.bfloat16)

            @pl.when(i < slabs - 1)
            def _():
                y_copy(v, p, me).start()

        strips[v][me] = images[v, me]

    def slot_copy(src, dst, send, recv, step):
        span = pl.ds(SLOT_BASE[step], SLOT_COUNT[step])
        n = STEPS.index(step)
        return pltpu.make_async_remote_copy(
            src_ref=src.at[span],
            dst_ref=dst.at[span],
            send_sem=send.at[n],
            recv_sem=recv.at[n],
            device_id=here + step,
            device_id_type=LOGICAL,
        )

    def c_copy(v, step):
        if v == views:
            src, dst = veil_outgoing, veil_landed
        else:
            src, dst = outgoing.at[v], landed[v]
        return slot_copy(src, dst, c_send.at[v], c_recv.at[v], step)

    def send_to(v, step):
        if step == 0:
            return

        @pl.when((col + step >= 0) & (col + step < columns))
        def _():
            c_copy(v, step).start()

    def await_from(v):
        for step in STEPS:
            if step == 0:
                continue

            @pl.when((col - step >= 0) & (col - step < columns))
            def _(step=step):
                c_copy(v, step).wait_recv()

    def place(v, n, put_left, put_right, read):
        step = STEPS[n]
        after = step + 1
        for member in (0, 1):
            piece = read(picks[v, n, member, 0])
            left = jnp.where(lane >= picks[v, n, member, 1], 1.0, 0.0).astype(jnp.bfloat16)
            right = jnp.where(lane < picks[v, n, member, 2], 1.0, 0.0).astype(jnp.bfloat16)
            put_left(step == 0, SLOT_BASE[step] + member, piece * left)
            put_right(
                after == 0, SLOT_BASE[after] + (2 if after < 4 else 0) + member, piece * right
            )

    ORDER = (4, 3, 2, 1, 0)

    all_o().wait_recv()

    for n in ORDER:
        for v in range(views):

            def put(own, slot, value, v=v):
                (veil_landed if own else veil_outgoing)[slot, v] = value

            place(v, n, put, put, lambda slab, v=v: veil_strips[slab, v])
        send_to(views, STEPS[n] + 1)
    send_to(views, -1)
    veil_landed[EMPTY] = jnp.zeros(veil_landed.shape[1:], jnp.bfloat16)

    for v in range(views):
        landed[v][EMPTY] = jnp.zeros(landed[v].shape[1:], jnp.bfloat16)

        all_y(v).wait_recv()

        for n in ORDER:

            def put(own, slot, value, v=v):
                if own:
                    landed[v][slot] = value
                else:
                    outgoing[v, slot] = value

            place(v, n, put, put, lambda slab, v=v: strips[v][slab])
            send_to(v, STEPS[n] + 1)
        send_to(v, -1)

    all_a().wait_send()
    all_b().wait_send()
    all_o().wait_send()
    for v in range(views):
        all_y(v).wait_send()

    await_from(views)
    for v in range(views):
        await_from(v)
        if v == views - 1:
            for w in range(views + 1):
                for step in STEPS:
                    if step == 0:
                        continue

                    @pl.when((col + step >= 0) & (col + step < columns))
                    def _(w=w, step=step):
                        c_copy(w, step).wait_send()

        def at_position(position, state, v=v):
            slab = slab_order[v, position]
            red, green, blue, transmit = state
            for n in reversed(range(len(STEPS))):
                slot = table[v, n, slab]
                piece = landed[v][slot].astype(jnp.float32)
                red = red + transmit * piece[0]
                green = green + transmit * piece[1]
                blue = blue + transmit * piece[2]
                veil = veil_landed[slot, v].astype(jnp.float32)
                transmit = transmit * (1.0 - veil)
            return red, green, blue, transmit

        zero = jnp.zeros((strip, lanes), jnp.float32)
        red, green, blue, transmit = lax.fori_loop(
            0, slabs, at_position, (zero, zero, zero, zero + 1.0), unroll=2
        )
        out_ref[v, 0, 0] = red
        out_ref[v, 1, 0] = green
        out_ref[v, 2, 0] = blue
        out_ref[v, 3, 0] = 1.0 - transmit


def on_device(density, albedo, targets, offsets, slab_order):
    depth_cells, rows, lanes = density.shape
    views = slab_order.shape[0]
    slabs = lax.axis_size("depth")
    columns = lax.axis_size("col")
    strip = rows // slabs
    terms = sum(len(shear_plan(shear, depth_cells)[1]) for shear in SHEARS)
    f32, bf16 = jnp.float32, jnp.bfloat16
    dma = pltpu.SemaphoreType.DMA
    return pl.pallas_call(
        functools.partial(kernel, (slabs, columns, depth_cells, rows, lanes)),
        out_shape=pltpu.VMEM((views, 4, 1, strip, lanes), f32),
        in_specs=[
            pl.BlockSpec(memory_space=pl.ANY),
            pl.BlockSpec(memory_space=pl.ANY),
            pl.BlockSpec(memory_space=pl.ANY),
            pl.BlockSpec(memory_space=pl.ANY),
            pl.BlockSpec(memory_space=pl.ANY),
        ],
        out_specs=pl.BlockSpec(memory_space=pltpu.VMEM),
        scratch_shapes=[
            pltpu.SMEM((views, slabs, 1, columns), jnp.int32),
            pltpu.SMEM((views, 1, 1, slabs), jnp.int32),
            pltpu.SMEM((views, slabs), jnp.int32),
            pltpu.VMEM((depth_cells, rows, lanes), f32),
            pltpu.VMEM((3, depth_cells, rows, lanes), bf16),
            pltpu.VMEM((slabs, strip, lanes), bf16),
            pltpu.VMEM((slabs, strip, lanes), bf16),
            pltpu.VMEM((slabs, strip, lanes), bf16),
            pltpu.VMEM((slabs, strip, lanes), bf16),
            pltpu.VMEM((terms, 3, rows, lanes), f32),
            pltpu.VMEM((views, slabs, 3, strip, lanes), bf16),
            pltpu.VMEM((slabs, views, strip, lanes), bf16),
            pltpu.VMEM((slabs, 3, strip, lanes), bf16),
            pltpu.VMEM((slabs, 3, strip, lanes), bf16),
            pltpu.VMEM((slabs, views, strip, lanes), bf16),
            pltpu.VMEM((views, SLOTS, 3, strip, lanes), bf16),
            pltpu.VMEM((SLOTS, views, strip, lanes), bf16),
            pltpu.VMEM((SLOTS + 1, 3, strip, lanes), bf16),
            pltpu.VMEM((SLOTS + 1, 3, strip, lanes), bf16),
            pltpu.VMEM((SLOTS + 1, views, strip, lanes), bf16),
            pltpu.SMEM((views, len(STEPS), slabs), jnp.int32),
            pltpu.SMEM((views, len(STEPS) - 1, 2, 3), jnp.int32),
            dma((slabs,)),
            dma((4,)),
            dma,
            dma,
            dma,
            dma,
            dma,
            dma,
            dma((views,)),
            dma((views,)),
            dma((views + 1, len(STEPS))),
            dma((views + 1, len(STEPS))),
        ],
        compiler_params=pltpu.CompilerParams(collective_id=0, has_side_effects=True),
    )(density, albedo, targets, offsets.transpose(0, 2, 3, 1), slab_order)


def solution(mesh):
    in_specs = (
        P("depth", "row", "col"),
        P(None, "depth", "row", "col"),
        P(None, None, "row", None),
        P(None, None, "row", "col"),
        P(),
    )
    out_specs = P(None, None, "row", "depth", "col")
    return jax.shard_map(
        on_device, mesh=mesh, in_specs=in_specs, out_specs=out_specs, check_vma=False
    )
```

```python
import functools
import math

import jax
import jax.numpy as jnp
from jax import lax
from jax.experimental import pallas as pl
from jax.experimental.pallas import tpu as pltpu
from jax.sharding import PartitionSpec as P

SHEARS = (0.3125, -0.4375)
BRIGHTNESS = 4.0
LOGICAL = pl.DeviceIdType.LOGICAL
FAR_FIRST = (4, 3, 5, 2, 6, 1, 7)

STEPS = (-1, 0, 1, 2, 3, 4)
SLOT_COUNT = {-1: 2, 0: 4, 1: 4, 2: 4, 3: 4, 4: 2}
SLOT_BASE = {-1: 0, 0: 2, 1: 6, 2: 10, 3: 14, 4: 18}
SLOTS = 20
LAND_BASE = {-1: 0, 0: 3, 1: 8, 2: 13, 3: 18, 4: 23}
LAND_SLOTS = 26
EARLY = 3


def shear_plan(shear, depth_cells):
    plan = []
    for z in range(depth_cells):
        whole = math.floor(shear * z)
        plan.append((whole, shear * z - whole))
    terms = sorted({k + e for k, f in plan for e in (0, 1) if e == 0 or f > 0})
    return plan, terms


def kernel(
    sizes,
    density_hbm,
    albedo_hbm,
    targets_hbm,
    offsets_hbm,
    order_hbm,
    out_ref,
    targets,
    offsets,
    slab_order,
    dens,
    alb,
    depth_strips,
    depth_seen,
    light_strips,
    light,
    partial,
    images,
    veils,
    strips_a,
    strips_b,
    veil_strips,
    outgoing,
    veil_outgoing,
    landed_a,
    landed_b,
    veil_landed,
    weights,
    table,
    picks,
    density_sems,
    load_sems,
    a_send,
    a_recv,
    b_send,
    b_recv,
    o_send,
    o_recv,
    y_send,
    y_recv,
    c_send,
    c_recv,
):
    slabs, columns, depth_cells, rows, lanes = sizes
    views = len(SHEARS)
    strips, landed = (strips_a, strips_b), (landed_a, landed_b)
    strip = rows // slabs
    plans = [shear_plan(shear, depth_cells) for shear in SHEARS]
    firsts = [0, len(plans[0][1])]
    me = lax.axis_index("depth")
    col = lax.axis_index("col")
    layer = lax.axis_size("row") * columns
    here = me * layer + lax.axis_index("row") * columns + col

    def device(peer):
        return here + (peer - me) * layer


    barrier = pltpu.get_barrier_semaphore()
    for hop in FAR_FIRST:
        pl.semaphore_signal(
            barrier,
            inc=1,
            device_id=device(lax.rem(me + hop, slabs)),
            device_id_type=LOGICAL,
        )
    for hop in (-4, -3, -2, -1, 1, 2, 3, 4):

        @pl.when((col + hop >= 0) & (col + hop < columns))
        def _(hop=hop):
            pl.semaphore_signal(barrier, inc=1, device_id=here + hop, device_id_type=LOGICAL)

    lane = lax.broadcasted_iota(jnp.int32, (strip, lanes), 1)

    def strip_rows(p):
        return pl.ds(pl.multiple_of(p * strip, strip), strip)

    def peer_at(i):
        half, sign = (i + 1) // 2, 1 - 2 * (i % 2)
        return lax.rem(me + slabs // 2 + sign * half, slabs)

    def density_load(i):
        at = strip_rows(peer_at(i))
        return pltpu.make_async_copy(density_hbm.at[:, at], dens.at[:, at], density_sems.at[i])

    @pl.loop(0, slabs)
    def _(i):
        density_load(i).start()

    load_small = [
        pltpu.make_async_copy(src, dst, load_sems.at[n])
        for n, (src, dst) in enumerate(
            ((offsets_hbm, offsets), (targets_hbm, targets), (order_hbm, slab_order))
        )
    ]
    for load in load_small:
        load.start()
    load_albedo = pltpu.make_async_copy(albedo_hbm, alb, load_sems.at[3])
    load_albedo.start()

    for n, step in enumerate(STEPS):
        count = SLOT_COUNT[step]
        for v in range(views):
            landed[v][n][count] = jnp.zeros(landed[v][n].shape[1:], jnp.bfloat16)
        veil_landed[LAND_BASE[step] + count] = jnp.zeros(veil_landed.shape[1:], jnp.bfloat16)

    neighbours = jnp.minimum(col, 4) + jnp.minimum(columns - 1 - col, 4)
    pl.semaphore_wait(barrier, slabs - 1 + neighbours)

    def depth_copy(src, dst, send_sem, recv_sem, peer):
        return pltpu.make_async_remote_copy(
            src_ref=src,
            dst_ref=dst,
            send_sem=send_sem,
            recv_sem=recv_sem,
            device_id=device(peer),
            device_id_type=LOGICAL,
        )

    def all_peers(src, dst, send_sem, recv_sem):
        span = pl.ds(0, slabs - 1)
        return depth_copy(src.at[span], dst.at[span], send_sem, recv_sem, me)

    def a_copy(peer, source):
        return depth_copy(depth_strips.at[peer], depth_seen.at[source], a_send, a_recv, peer)

    def b_copy(peer, source):
        return depth_copy(
            light_strips.at[peer], light.at[source], b_send, b_recv.at[source], peer
        )

    def all_a():
        return all_peers(depth_strips, depth_seen, a_send, a_recv)

    def all_b():
        return all_peers(light_strips, light, b_send, b_recv.at[0])

    @pl.loop(0, slabs)
    def _(i):
        p = peer_at(i)
        density_load(i).wait()
        total = jnp.sum(dens[:, strip_rows(p), :], axis=0)
        depth_strips[p] = total

        @pl.when(i < slabs - 1)
        def _():
            a_copy(p, me).start()

    depth_seen[me] = depth_strips[me]
    for load in load_small:
        load.wait()
    load_albedo.wait()

    def lane_mask(shift, weight):
        inside = (lane >= shift) if shift >= 0 else (lane < lanes + shift)
        return jnp.where(inside, jnp.float32(weight), jnp.float32(0.0))

    def rolled(value, shift):
        return value if shift % lanes == 0 else pltpu.roll(value, shift % lanes, 1)

    def o_copy(peer, source):
        return depth_copy(veils.at[peer], veil_strips.at[source], o_send, o_recv, peer)

    def composite(i):
        p = peer_at(i)
        at = strip_rows(p)
        inside = jnp.ones((strip, lanes), jnp.float32)
        transmit = [jnp.ones((strip, lanes), jnp.float32) for _ in range(views)]
        sums = [{} for _ in range(views)]
        for z in range(depth_cells):
            through = jnp.exp(-dens[z, at, :])
            opacity = 1.0 - through
            lit = (BRIGHTNESS * inside) * opacity
            inside = inside * through
            colour = [alb[c, z, at, :].astype(jnp.float32) * lit for c in range(3)]
            for v in range(views):
                whole, fraction = plans[v][0][z]
                moved = None
                for k, weight in ((whole, 1.0 - fraction), (whole + 1, fraction)):
                    if weight == 0.0:
                        continue
                    part = lane_mask(k, weight) * rolled(opacity, k)
                    moved = part if moved is None else moved + part
                    seen = transmit[v] if z else None
                    seen = lane_mask(-k, weight) * (
                        rolled(seen, -k) if z else jnp.ones((strip, lanes), jnp.float32)
                    )
                    terms = [seen * colour[c] for c in range(3)]
                    if k in sums[v]:
                        terms = [old + new for old, new in zip(sums[v][k], terms)]
                    sums[v][k] = terms
                transmit[v] = transmit[v] * (1.0 - moved)
                later = {
                    k for w, f in plans[v][0][z + 1 :] for k in ((w, w + 1) if f else (w,))
                }
                for k in [k for k in sums[v] if k not in later]:
                    for c in range(3):
                        partial[firsts[v] + plans[v][1].index(k), c, at, :] = sums[v][k][c]
                    del sums[v][k]
        for v in range(views):
            image = pltpu.roll(1.0 - transmit[v], offsets[v, 0, 0, me], 1)
            veils[p, v] = image.astype(jnp.bfloat16)

        @pl.when(i < slabs - 1)
        def _():
            o_copy(p, me).start()

    pl.loop(0, EARLY)(composite)
    all_a().wait_recv()
    before = jnp.zeros((strip, lanes), jnp.float32)
    for d in range(slabs):
        light_strips[d] = jnp.exp(-before)
        before = before + depth_seen[d]

    @pl.loop(0, slabs - 1)
    def _(i):
        b_copy(peer_at(i), me).start()

    light[me] = light_strips[me]
    pl.loop(EARLY, slabs)(composite)
    veil_strips[me] = veils[me]

    for v in range(views):
        rel = [targets[v, d, 0, col] - col for d in range(slabs)]
        for n, step in enumerate(STEPS[:-1]):
            first = jnp.int32(slabs)
            second = jnp.int32(-1)
            for d in range(slabs):
                match = rel[d] == step
                first = jnp.where(match, jnp.minimum(first, d), first)
                second = jnp.where(match, d, second)
            valid = second >= 0
            for member, slab in ((0, first), (1, second)):
                slab = jnp.where(valid, slab, 0)
                start = offsets[v, 0, 0, slab]
                picks[v, n, member, 0] = slab
                picks[v, n, member, 1] = jnp.where(valid, start, lanes)
                picks[v, n, member, 2] = jnp.where(valid, start, 0)

    for v in range(views):
        for n, step in enumerate(STEPS):
            source = col - step
            present = (source >= 0) & (source < columns)
            source = jnp.clip(source, 0, columns - 1)
            rel = [targets[v, d, 0, source] - source for d in range(slabs)]
            empty = SLOT_COUNT[step]
            for d in range(slabs):
                second = functools.reduce(
                    jnp.logical_or, [rel[e] == rel[d] for e in range(d)], False
                )
                member = jnp.where(second, 1, 0)
                slot = jnp.int32(empty)
                if step < 4:
                    slot = jnp.where(rel[d] == step, member, slot)
                if step > -1:
                    slot = jnp.where(rel[d] == step - 1, member + (2 if step < 4 else 0), slot)
                table[v, n, d] = jnp.where(present, slot, empty)

    def y_copy(v, peer, source):
        return depth_copy(
            images.at[v, peer], strips[v].at[source], y_send.at[v], y_recv.at[v], peer
        )

    def all_o():
        return all_peers(veils, veil_strips, o_send, o_recv)

    def all_y(v):
        return all_peers(images.at[v], strips[v], y_send.at[v], y_recv.at[v])

    def colours(v, p):
        at = strip_rows(p)
        front_light = light[p]
        for c in range(3):
            total = None
            for n, k in enumerate(plans[v][1]):
                part = rolled(front_light * partial[firsts[v] + n, c, at, :], k)
                total = part if total is None else total + part
            total = pltpu.roll(total, offsets[v, 0, 0, me], 1)
            images[v, p, c] = total.astype(jnp.bfloat16)

    @pl.loop(0, slabs - 1)
    def _(i):
        b_copy(me, peer_at(i)).wait_recv()

    for v in range(views):

        @pl.loop(0, slabs, unroll=2)
        def _(i, v=v):
            p = peer_at(i)
            colours(v, p)

            @pl.when(i < slabs - 1)
            def _():
                y_copy(v, p, me).start()

        strips[v][me] = images[v, me]

    def c_copy(v, step):
        n, count = STEPS.index(step), SLOT_COUNT[step]
        span = pl.ds(SLOT_BASE[step], count)
        if v == views:
            src, dst = veil_outgoing.at[span], veil_landed.at[pl.ds(LAND_BASE[step], count)]
        else:
            src, dst = outgoing.at[v, span], landed[v][n].at[pl.ds(0, count)]
        return pltpu.make_async_remote_copy(
            src_ref=src,
            dst_ref=dst,
            send_sem=c_send.at[v, n],
            recv_sem=c_recv.at[v, n],
            device_id=here + step,
            device_id_type=LOGICAL,
        )

    def send_to(v, step):
        if step == 0:
            return

        @pl.when((col + step >= 0) & (col + step < columns))
        def _():
            c_copy(v, step).start()

    def await_from(v, step):
        if step == 0:
            return

        @pl.when((col - step >= 0) & (col - step < columns))
        def _():
            c_copy(v, step).wait_recv()

    def place(v, n, put_left, put_right, read):
        step = STEPS[n]
        after = step + 1
        for member in (0, 1):
            piece = read(picks[v, n, member, 0])
            left = jnp.where(lane >= picks[v, n, member, 1], 1.0, 0.0).astype(jnp.bfloat16)
            right = jnp.where(lane < picks[v, n, member, 2], 1.0, 0.0).astype(jnp.bfloat16)
            put_left(step, member, piece * left)
            put_right(after, member + (2 if after < 4 else 0), piece * right)

    ORDER = ((3, ()), (2, (2,)), (4, (3, 4)), (1, (1,)), (0, (-1,)))

    all_o().wait_recv()

    for n, ready in ORDER:
        for v in range(views):

            def put(step, slot, value, v=v):
                if step == 0:
                    veil_landed[LAND_BASE[step] + slot, v] = value
                else:
                    veil_outgoing[SLOT_BASE[step] + slot, v] = value

            place(v, n, put, put, lambda slab, v=v: veil_strips[slab, v])
        for step in ready:
            send_to(views, step)
    for v in range(views):
        all_y(v).wait_recv()

        for n, ready in ORDER:

            def put(step, slot, value, v=v):
                if step == 0:
                    landed[v][STEPS.index(step)][slot] = value
                else:
                    outgoing[v, SLOT_BASE[step] + slot] = value

            place(v, n, put, put, lambda slab, v=v: strips[v][slab])
            for step in ready:
                send_to(v, step)

    all_a().wait_send()
    all_b().wait_send()
    all_o().wait_send()
    for v in range(views):
        all_y(v).wait_send()

    for step in STEPS:
        await_from(views, step)
    for v in range(views):

        def at_position(position, transmit, v=v):
            slab = slab_order[v, position]
            for n, step in reversed(list(enumerate(STEPS))):
                weights[v, n, position] = transmit
                veil = veil_landed[LAND_BASE[step] + table[v, n, slab], v]
                transmit = transmit * (1.0 - veil.astype(jnp.float32))
            return transmit

        one = jnp.ones((strip, lanes), jnp.float32)
        out_ref[v, 3, 0] = 1.0 - lax.fori_loop(0, slabs, at_position, one, unroll=2)

    for w in range(views + 1):
        for step in STEPS:
            if step == 0:
                continue

            @pl.when((col + step >= 0) & (col + step < columns))
            def _(w=w, step=step):
                c_copy(w, step).wait_send()

    for v in range(views):
        zero = jnp.zeros((strip, lanes), jnp.float32)
        sums = (zero, zero, zero)
        for step in (0, -1, 1, 4, 3, 2):
            n = STEPS.index(step)
            await_from(v, step)

            def add_piece(position, sums, v=v, n=n):
                piece = landed[v][n][table[v, n, slab_order[v, position]]].astype(jnp.float32)
                weight = weights[v, n, position]
                return tuple(total + weight * piece[c] for c, total in enumerate(sums))

            sums = lax.fori_loop(0, slabs, add_piece, sums, unroll=8)
        for c in range(3):
            out_ref[v, c, 0] = sums[c]


def on_device(density, albedo, targets, offsets, slab_order):
    depth_cells, rows, lanes = density.shape
    views = slab_order.shape[0]
    slabs = lax.axis_size("depth")
    columns = lax.axis_size("col")
    strip = rows // slabs
    terms = sum(len(shear_plan(shear, depth_cells)[1]) for shear in SHEARS)
    f32, bf16 = jnp.float32, jnp.bfloat16
    dma = pltpu.SemaphoreType.DMA
    return pl.pallas_call(
        functools.partial(kernel, (slabs, columns, depth_cells, rows, lanes)),
        out_shape=pltpu.VMEM((views, 4, 1, strip, lanes), f32),
        in_specs=[
            pl.BlockSpec(memory_space=pl.ANY),
            pl.BlockSpec(memory_space=pl.ANY),
            pl.BlockSpec(memory_space=pl.ANY),
            pl.BlockSpec(memory_space=pl.ANY),
            pl.BlockSpec(memory_space=pl.ANY),
        ],
        out_specs=pl.BlockSpec(memory_space=pltpu.VMEM),
        scratch_shapes=[
            pltpu.SMEM((views, slabs, 1, columns), jnp.int32),
            pltpu.SMEM((views, 1, 1, slabs), jnp.int32),
            pltpu.SMEM((views, slabs), jnp.int32),
            pltpu.VMEM((depth_cells, rows, lanes), f32),
            pltpu.VMEM((3, depth_cells, rows, lanes), bf16),
            pltpu.VMEM((slabs, strip, lanes), f32),
            pltpu.VMEM((slabs, strip, lanes), f32),
            pltpu.VMEM((slabs, strip, lanes), f32),
            pltpu.VMEM((slabs, strip, lanes), f32),
            pltpu.VMEM((terms, 3, rows, lanes), f32),
            pltpu.VMEM((views, slabs, 3, strip, lanes), bf16),
            pltpu.VMEM((slabs, views, strip, lanes), bf16),
            pltpu.VMEM((slabs, 3, strip, lanes), bf16),
            pltpu.VMEM((slabs, 3, strip, lanes), bf16),
            pltpu.VMEM((slabs, views, strip, lanes), bf16),
            pltpu.VMEM((views, SLOTS, 3, strip, lanes), bf16),
            pltpu.VMEM((SLOTS, views, strip, lanes), bf16),
            [pltpu.VMEM((SLOT_COUNT[step] + 1, 3, strip, lanes), bf16) for step in STEPS],
            [pltpu.VMEM((SLOT_COUNT[step] + 1, 3, strip, lanes), bf16) for step in STEPS],
            pltpu.VMEM((LAND_SLOTS, views, strip, lanes), bf16),
            pltpu.VMEM((views, len(STEPS), slabs, strip, lanes), f32),
            pltpu.SMEM((views, len(STEPS), slabs), jnp.int32),
            pltpu.SMEM((views, len(STEPS) - 1, 2, 3), jnp.int32),
            dma((slabs,)),
            dma((4,)),
            dma,
            dma,
            dma,
            dma((slabs,)),
            dma,
            dma,
            dma((views,)),
            dma((views,)),
            dma((views + 1, len(STEPS))),
            dma((views + 1, len(STEPS))),
        ],
        compiler_params=pltpu.CompilerParams(collective_id=0, has_side_effects=True),
    )(density, albedo, targets, offsets.transpose(0, 2, 3, 1), slab_order)


def solution(mesh):
    in_specs = (
        P("depth", "row", "col"),
        P(None, "depth", "row", "col"),
        P(None, None, "row", None),
        P(None, None, "row", "col"),
        P(),
    )
    out_specs = P(None, None, "row", "depth", "col")
    return jax.shard_map(
        on_device, mesh=mesh, in_specs=in_specs, out_specs=out_specs, check_vma=False
    )
```

```python
import functools
import math

import jax
import jax.numpy as jnp
from jax import lax
from jax.experimental import pallas as pl
from jax.experimental.pallas import tpu as pltpu
from jax.sharding import PartitionSpec as P

SHEARS = (0.3125, -0.4375)
BRIGHTNESS = 4.0
LOGICAL = pl.DeviceIdType.LOGICAL
FAR_FIRST = (4, 3, 5, 2, 6, 1, 7)

STEPS = (-1, 0, 1, 2, 3, 4)
SLOT_COUNT = {-1: 2, 0: 4, 1: 4, 2: 4, 3: 4, 4: 2}
SLOT_BASE = {-1: 0, 0: 2, 1: 6, 2: 10, 3: 14, 4: 18}
SLOTS = 20
LAND_BASE = {-1: 0, 0: 3, 1: 8, 2: 13, 3: 18, 4: 23}
LAND_SLOTS = 26
EARLY = 3


def shear_plan(shear, depth_cells):
    plan = []
    for z in range(depth_cells):
        whole = math.floor(shear * z)
        plan.append((whole, shear * z - whole))
    terms = sorted({k + e for k, f in plan for e in (0, 1) if e == 0 or f > 0})
    return plan, terms


def kernel(
    sizes,
    density_hbm,
    albedo_hbm,
    targets_hbm,
    offsets_hbm,
    order_hbm,
    out_ref,
    targets,
    offsets,
    slab_order,
    dens,
    alb,
    depth_strips,
    depth_seen,
    light_strips,
    light,
    partial,
    images,
    veils,
    strips_a,
    strips_b,
    veil_strips,
    outgoing,
    veil_outgoing,
    landed_a,
    landed_b,
    veil_landed,
    weights,
    table,
    picks,
    density_sems,
    load_sems,
    a_send,
    a_recv,
    b_send,
    b_recv,
    o_send,
    o_recv,
    y_send,
    y_recv,
    c_send,
    c_recv,
):
    slabs, columns, depth_cells, rows, lanes = sizes
    views = len(SHEARS)
    strips, landed = (strips_a, strips_b), (landed_a, landed_b)
    strip = rows // slabs
    plans = [shear_plan(shear, depth_cells) for shear in SHEARS]
    firsts = [0, len(plans[0][1])]
    me = lax.axis_index("depth")
    col = lax.axis_index("col")
    layer = lax.axis_size("row") * columns
    here = me * layer + lax.axis_index("row") * columns + col

    def device(peer):
        return here + (peer - me) * layer


    barrier = pltpu.get_barrier_semaphore()
    for hop in FAR_FIRST:
        pl.semaphore_signal(
            barrier,
            inc=1,
            device_id=device(lax.rem(me + hop, slabs)),
            device_id_type=LOGICAL,
        )
    for hop in (-4, -3, -2, -1, 1, 2, 3, 4):

        @pl.when((col + hop >= 0) & (col + hop < columns))
        def _(hop=hop):
            pl.semaphore_signal(barrier, inc=1, device_id=here + hop, device_id_type=LOGICAL)

    lane = lax.broadcasted_iota(jnp.int32, (strip, lanes), 1)

    def strip_rows(p):
        return pl.ds(pl.multiple_of(p * strip, strip), strip)

    def peer_at(i):
        half, sign = (i + 1) // 2, 1 - 2 * (i % 2)
        return lax.rem(me + slabs // 2 + sign * half, slabs)

    def density_load(i):
        at = strip_rows(peer_at(i))
        return pltpu.make_async_copy(density_hbm.at[:, at], dens.at[:, at], density_sems.at[i])

    @pl.loop(0, slabs)
    def _(i):
        density_load(i).start()

    load_small = [
        pltpu.make_async_copy(src, dst, load_sems.at[n])
        for n, (src, dst) in enumerate(
            ((offsets_hbm, offsets), (targets_hbm, targets), (order_hbm, slab_order))
        )
    ]
    for load in load_small:
        load.start()
    load_albedo = pltpu.make_async_copy(albedo_hbm, alb, load_sems.at[3])
    load_albedo.start()

    for n, step in enumerate(STEPS):
        count = SLOT_COUNT[step]
        for v in range(views):
            landed[v][n][count] = jnp.zeros(landed[v][n].shape[1:], jnp.bfloat16)
        veil_landed[LAND_BASE[step] + count] = jnp.zeros(veil_landed.shape[1:], jnp.bfloat16)

    neighbours = jnp.minimum(col, 4) + jnp.minimum(columns - 1 - col, 4)
    pl.semaphore_wait(barrier, slabs - 1 + neighbours)

    def depth_copy(src, dst, send_sem, recv_sem, peer):
        return pltpu.make_async_remote_copy(
            src_ref=src,
            dst_ref=dst,
            send_sem=send_sem,
            recv_sem=recv_sem,
            device_id=device(peer),
            device_id_type=LOGICAL,
        )

    def all_peers(src, dst, send_sem, recv_sem):
        span = pl.ds(0, slabs - 1)
        return depth_copy(src.at[span], dst.at[span], send_sem, recv_sem, me)

    def a_copy(peer, source):
        return depth_copy(depth_strips.at[peer], depth_seen.at[source], a_send, a_recv, peer)

    def b_copy(peer, source):
        return depth_copy(
            light_strips.at[peer], light.at[source], b_send, b_recv.at[source], peer
        )

    def all_a():
        return all_peers(depth_strips, depth_seen, a_send, a_recv)

    def all_b():
        return all_peers(light_strips, light, b_send, b_recv.at[0])

    @pl.loop(0, slabs)
    def _(i):
        p = peer_at(i)
        density_load(i).wait()
        total = jnp.sum(dens[:, strip_rows(p), :], axis=0)
        depth_strips[p] = total

        @pl.when(i < slabs - 1)
        def _():
            a_copy(p, me).start()

    depth_seen[me] = depth_strips[me]
    for load in load_small:
        load.wait()
    load_albedo.wait()

    def lane_mask(shift, weight):
        inside = (lane >= shift) if shift >= 0 else (lane < lanes + shift)
        return jnp.where(inside, jnp.float32(weight), jnp.float32(0.0))

    def rolled(value, shift):
        return value if shift % lanes == 0 else pltpu.roll(value, shift % lanes, 1)

    def o_copy(peer, source):
        return depth_copy(veils.at[peer], veil_strips.at[source], o_send, o_recv, peer)

    def composite(i):
        p = peer_at(i)
        at = strip_rows(p)
        inside = jnp.ones((strip, lanes), jnp.float32)
        transmit = [jnp.ones((strip, lanes), jnp.float32) for _ in range(views)]
        sums = [{} for _ in range(views)]
        for z in range(depth_cells):
            through = jnp.exp(-dens[z, at, :])
            opacity = 1.0 - through
            lit = (BRIGHTNESS * inside) * opacity
            inside = inside * through
            colour = [alb[c, z, at, :].astype(jnp.float32) * lit for c in range(3)]
            for v in range(views):
                whole, fraction = plans[v][0][z]
                moved = None
                for k, weight in ((whole, 1.0 - fraction), (whole + 1, fraction)):
                    if weight == 0.0:
                        continue
                    part = lane_mask(k, weight) * rolled(opacity, k)
                    moved = part if moved is None else moved + part
                    seen = transmit[v] if z else None
                    seen = lane_mask(-k, weight) * (
                        rolled(seen, -k) if z else jnp.ones((strip, lanes), jnp.float32)
                    )
                    terms = [seen * colour[c] for c in range(3)]
                    if k in sums[v]:
                        terms = [old + new for old, new in zip(sums[v][k], terms)]
                    sums[v][k] = terms
                transmit[v] = transmit[v] * (1.0 - moved)
                later = {
                    k for w, f in plans[v][0][z + 1 :] for k in ((w, w + 1) if f else (w,))
                }
                for k in [k for k in sums[v] if k not in later]:
                    for c in range(3):
                        partial[firsts[v] + plans[v][1].index(k), c, at, :] = sums[v][k][c]
                    del sums[v][k]
        for v in range(views):
            image = pltpu.roll(1.0 - transmit[v], offsets[v, 0, 0, me], 1)
            veils[p, v] = image.astype(jnp.bfloat16)

        @pl.when(i < slabs - 1)
        def _():
            o_copy(p, me).start()

    pl.loop(0, EARLY)(composite)
    all_a().wait_recv()
    before = jnp.zeros((strip, lanes), jnp.float32)
    for d in range(slabs):
        light_strips[d] = jnp.exp(-before)
        before = before + depth_seen[d]

    for i in range(slabs - 1):
        b_copy(peer_at(i), me).start()

    light[me] = light_strips[me]
    pl.loop(EARLY, slabs)(composite)
    veil_strips[me] = veils[me]

    for v in range(views):
        rel = [targets[v, d, 0, col] - col for d in range(slabs)]
        for n, step in enumerate(STEPS[:-1]):
            first = jnp.int32(slabs)
            second = jnp.int32(-1)
            for d in range(slabs):
                match = rel[d] == step
                first = jnp.where(match, jnp.minimum(first, d), first)
                second = jnp.where(match, d, second)
            valid = second >= 0
            for member, slab in ((0, first), (1, second)):
                slab = jnp.where(valid, slab, 0)
                start = offsets[v, 0, 0, slab]
                picks[v, n, member, 0] = slab
                picks[v, n, member, 1] = jnp.where(valid, start, lanes)
                picks[v, n, member, 2] = jnp.where(valid, start, 0)

    for v in range(views):
        for n, step in enumerate(STEPS):
            source = col - step
            present = (source >= 0) & (source < columns)
            source = jnp.clip(source, 0, columns - 1)
            rel = [targets[v, d, 0, source] - source for d in range(slabs)]
            empty = SLOT_COUNT[step]
            for d in range(slabs):
                second = functools.reduce(
                    jnp.logical_or, [rel[e] == rel[d] for e in range(d)], False
                )
                member = jnp.where(second, 1, 0)
                slot = jnp.int32(empty)
                if step < 4:
                    slot = jnp.where(rel[d] == step, member, slot)
                if step > -1:
                    slot = jnp.where(rel[d] == step - 1, member + (2 if step < 4 else 0), slot)
                table[v, n, d] = jnp.where(present, slot, empty)

    def y_copy(v, peer, source):
        return depth_copy(
            images.at[v, peer], strips[v].at[source], y_send.at[v], y_recv.at[v], peer
        )

    def all_o():
        return all_peers(veils, veil_strips, o_send, o_recv)

    def all_y(v):
        return all_peers(images.at[v], strips[v], y_send.at[v], y_recv.at[v])

    def colours(v, p):
        at = strip_rows(p)
        front_light = light[p]
        for c in range(3):
            total = None
            for n, k in enumerate(plans[v][1]):
                part = rolled(front_light * partial[firsts[v] + n, c, at, :], k)
                total = part if total is None else total + part
            total = pltpu.roll(total, offsets[v, 0, 0, me], 1)
            images[v, p, c] = total.astype(jnp.bfloat16)

    for i in range(slabs - 1):
        b_copy(me, peer_at(i)).wait_recv()

    for v in range(views):

        @pl.loop(0, slabs, unroll=2)
        def _(i, v=v):
            p = peer_at(i)
            colours(v, p)

            @pl.when(i < slabs - 1)
            def _():
                y_copy(v, p, me).start()

        strips[v][me] = images[v, me]

    def c_copy(v, step):
        n, count = STEPS.index(step), SLOT_COUNT[step]
        span = pl.ds(SLOT_BASE[step], count)
        if v == views:
            src, dst = veil_outgoing.at[span], veil_landed.at[pl.ds(LAND_BASE[step], count)]
        else:
            src, dst = outgoing.at[v, span], landed[v][n].at[pl.ds(0, count)]
        return pltpu.make_async_remote_copy(
            src_ref=src,
            dst_ref=dst,
            send_sem=c_send.at[v, n],
            recv_sem=c_recv.at[v, n],
            device_id=here + step,
            device_id_type=LOGICAL,
        )

    def send_to(v, step):
        if step == 0:
            return

        @pl.when((col + step >= 0) & (col + step < columns))
        def _():
            c_copy(v, step).start()

    def await_from(v, step):
        if step == 0:
            return

        @pl.when((col - step >= 0) & (col - step < columns))
        def _():
            c_copy(v, step).wait_recv()

    def place(v, n, put_left, put_right, read):
        step = STEPS[n]
        after = step + 1
        for member in (0, 1):
            piece = read(picks[v, n, member, 0])
            left = jnp.where(lane >= picks[v, n, member, 1], 1.0, 0.0).astype(jnp.bfloat16)
            right = jnp.where(lane < picks[v, n, member, 2], 1.0, 0.0).astype(jnp.bfloat16)
            put_left(step, member, piece * left)
            put_right(after, member + (2 if after < 4 else 0), piece * right)

    ORDER = ((3, ()), (2, (2,)), (4, (3, 4)), (1, (1,)), (0, (-1,)))

    all_o().wait_recv()

    for n, ready in ORDER:
        for v in range(views):

            def put(step, slot, value, v=v):
                if step == 0:
                    veil_landed[LAND_BASE[step] + slot, v] = value
                else:
                    veil_outgoing[SLOT_BASE[step] + slot, v] = value

            place(v, n, put, put, lambda slab, v=v: veil_strips[slab, v])
        for step in ready:
            send_to(views, step)
    for v in range(views):
        all_y(v).wait_recv()

        for n, ready in ORDER:

            def put(step, slot, value, v=v):
                if step == 0:
                    landed[v][STEPS.index(step)][slot] = value
                else:
                    outgoing[v, SLOT_BASE[step] + slot] = value

            place(v, n, put, put, lambda slab, v=v: strips[v][slab])
            for step in ready:
                send_to(v, step)

    all_a().wait_send()
    all_b().wait_send()
    all_o().wait_send()
    for v in range(views):
        all_y(v).wait_send()

    for step in STEPS:
        await_from(views, step)
    for v in range(views):

        def at_position(position, transmit, v=v):
            slab = slab_order[v, position]
            for n, step in reversed(list(enumerate(STEPS))):
                weights[v, n, position] = transmit
                veil = veil_landed[LAND_BASE[step] + table[v, n, slab], v]
                transmit = transmit * (1.0 - veil.astype(jnp.float32))
            return transmit

        one = jnp.ones((strip, lanes), jnp.float32)
        out_ref[v, 3, 0] = 1.0 - lax.fori_loop(0, slabs, at_position, one, unroll=2)

    for w in range(views + 1):
        for step in STEPS:
            if step == 0:
                continue

            @pl.when((col + step >= 0) & (col + step < columns))
            def _(w=w, step=step):
                c_copy(w, step).wait_send()

    for v in range(views):
        zero = jnp.zeros((strip, lanes), jnp.float32)
        sums = (zero, zero, zero)
        for step in (0, -1, 1, 4, 3, 2):
            n = STEPS.index(step)
            await_from(v, step)

            def add_piece(position, sums, v=v, n=n):
                piece = landed[v][n][table[v, n, slab_order[v, position]]].astype(jnp.float32)
                weight = weights[v, n, position]
                return tuple(total + weight * piece[c] for c, total in enumerate(sums))

            sums = lax.fori_loop(0, slabs, add_piece, sums, unroll=8)
        for c in range(3):
            out_ref[v, c, 0] = sums[c]


def on_device(density, albedo, targets, offsets, slab_order):
    depth_cells, rows, lanes = density.shape
    views = slab_order.shape[0]
    slabs = lax.axis_size("depth")
    columns = lax.axis_size("col")
    strip = rows // slabs
    terms = sum(len(shear_plan(shear, depth_cells)[1]) for shear in SHEARS)
    f32, bf16 = jnp.float32, jnp.bfloat16
    dma = pltpu.SemaphoreType.DMA
    return pl.pallas_call(
        functools.partial(kernel, (slabs, columns, depth_cells, rows, lanes)),
        out_shape=pltpu.VMEM((views, 4, 1, strip, lanes), f32),
        in_specs=[
            pl.BlockSpec(memory_space=pl.ANY),
            pl.BlockSpec(memory_space=pl.ANY),
            pl.BlockSpec(memory_space=pl.ANY),
            pl.BlockSpec(memory_space=pl.ANY),
            pl.BlockSpec(memory_space=pl.ANY),
        ],
        out_specs=pl.BlockSpec(memory_space=pltpu.VMEM),
        scratch_shapes=[
            pltpu.SMEM((views, slabs, 1, columns), jnp.int32),
            pltpu.SMEM((views, 1, 1, slabs), jnp.int32),
            pltpu.SMEM((views, slabs), jnp.int32),
            pltpu.VMEM((depth_cells, rows, lanes), f32),
            pltpu.VMEM((3, depth_cells, rows, lanes), bf16),
            pltpu.VMEM((slabs, strip, lanes), f32),
            pltpu.VMEM((slabs, strip, lanes), f32),
            pltpu.VMEM((slabs, strip, lanes), f32),
            pltpu.VMEM((slabs, strip, lanes), f32),
            pltpu.VMEM((terms, 3, rows, lanes), f32),
            pltpu.VMEM((views, slabs, 3, strip, lanes), bf16),
            pltpu.VMEM((slabs, views, strip, lanes), bf16),
            pltpu.VMEM((slabs, 3, strip, lanes), bf16),
            pltpu.VMEM((slabs, 3, strip, lanes), bf16),
            pltpu.VMEM((slabs, views, strip, lanes), bf16),
            pltpu.VMEM((views, SLOTS, 3, strip, lanes), bf16),
            pltpu.VMEM((SLOTS, views, strip, lanes), bf16),
            [pltpu.VMEM((SLOT_COUNT[step] + 1, 3, strip, lanes), bf16) for step in STEPS],
            [pltpu.VMEM((SLOT_COUNT[step] + 1, 3, strip, lanes), bf16) for step in STEPS],
            pltpu.VMEM((LAND_SLOTS, views, strip, lanes), bf16),
            pltpu.VMEM((views, len(STEPS), slabs, strip, lanes), f32),
            pltpu.SMEM((views, len(STEPS), slabs), jnp.int32),
            pltpu.SMEM((views, len(STEPS) - 1, 2, 3), jnp.int32),
            dma((slabs,)),
            dma((4,)),
            dma,
            dma,
            dma,
            dma((slabs,)),
            dma,
            dma,
            dma((views,)),
            dma((views,)),
            dma((views + 1, len(STEPS))),
            dma((views + 1, len(STEPS))),
        ],
        compiler_params=pltpu.CompilerParams(collective_id=0, has_side_effects=True),
    )(density, albedo, targets, offsets.transpose(0, 2, 3, 1), slab_order)


def solution(mesh):
    in_specs = (
        P("depth", "row", "col"),
        P(None, "depth", "row", "col"),
        P(None, None, "row", None),
        P(None, None, "row", "col"),
        P(),
    )
    out_specs = P(None, None, "row", "depth", "col")
    return jax.shard_map(
        on_device, mesh=mesh, in_specs=in_specs, out_specs=out_specs, check_vma=False
    )
```
